32 devices in a mesh: replica: 8 (over z, x), group: 4 (over y, core).
Axes of the slice: x: 2, y: 2, z: 4, core: 2. Of those that a mesh axis runs over, the one named last changes fastest.
Arguments:
- inputs: bfloat16 [8192, 576], P(('replica', 'group')), may hold values from -6 to 6
- segment_ids: int32 [32, 256], P(('replica', 'group')), may hold values from 0 to 2, never falling along the last dimension, each value on 1 to 128 neighbouring positions
- live_counts: int32 [32], P(('replica', 'group')), may hold values from 128 to 256, as said below
- cotangent: bfloat16 [8192, 576], P(('replica', 'group')), may hold values from -6 to 6
- w_query: bfloat16 [576, 576], P('group'), may hold values from -0.25 to 0.25
- w_key: bfloat16 [576, 192], P('group'), may hold values from -0.25 to 0.25
- w_value: bfloat16 [576, 192], P('group'), may hold values from -0.25 to 0.25
- w_out: bfloat16 [576, 576], P(None, 'group'), may hold values from -0.75 to 0.75
- w_gate: bfloat16 [576, 1536], P('group'), may hold values from -0.25 to 0.25
- w_up: bfloat16 [576, 1536], P('group'), may hold values from -0.25 to 0.25
- w_down: bfloat16 [1536, 576], P(None, 'group'), may hold values from -0.15625 to 0.15625
- norm_attn: bfloat16 [576], P('group'), may hold values from 0.5 to 1.5
- norm_ffn: bfloat16 [576], P('group'), may hold values from 0.5 to 1.5
Outputs:
- output: bfloat16 [8192, 576], P(('replica', 'group'))
- grad_input: float32 [8192, 576], P(('replica', 'group'))
- grad_query: float32 [576, 576], P('group')
- grad_key: float32 [576, 192], P('group')
- grad_value: float32 [576, 192], P('group')
- grad_out: float32 [576, 576], P(None, 'group')
- grad_gate: float32 [576, 1536], P('group')
- grad_up: float32 [576, 1536], P('group')
- grad_down: float32 [1536, 576], P(None, 'group')
- grad_norm_attn: float32 [576], P('group')
- grad_norm_ffn: float32 [576], P('group')
The draws below stay inside these ranges and needn't reach their ends.
Inputs may be any that keep to these rules, and one draw needn't show every extreme that they name: `segment_ids`: within each row the ids never fall; every id appears; each sequence has 1 to 128 slots and one has exactly 128. `live_counts`: some device is full and some holds exactly 128 real tokens.
All inputs are finite; a program needn't handle non-finite values.
Results may differ from the reference program's by a relative error of at most 0.012.
Values may be sent and summed in bfloat16 or wider, within the bound.
A program may use at most 128 MiB of HBM per device.

```python
import math
import jax
import jax.numpy as jnp
import numpy as np
from jax import lax

D = 576
HEADS = 9
KV_HEADS = 3
HEAD = 64
FF = 1536
TOK_DEV = 256
SEQ_MOST = 128
SEGS = 3
TOKENS = 8192
DEVICES = 32


def draw_live_counts(key, part):
    count_key = jax.random.fold_in(key, 83)
    counts = jax.random.randint(jax.random.fold_in(count_key, 1), (DEVICES,), TOK_DEV // 2, TOK_DEV + 1, jnp.int32)
    order = jax.random.permutation(jax.random.fold_in(count_key, 2), DEVICES)
    counts = counts.at[order[0]].set(TOK_DEV)
    counts = counts.at[order[1]].set(TOK_DEV // 2)
    return counts.astype(jnp.int32)


def level_of(stream_key, shape, pieces, least, high):
    def one(axis_at, parts):
        steps = jax.random.uniform(jax.random.fold_in(jax.random.fold_in(stream_key, 6), axis_at), (parts,), jnp.float32, least / len(pieces), high / len(pieces))
        return jnp.repeat(jnp.exp(steps), shape[axis_at] // parts).reshape((-1,) + (1,) * (len(shape) - axis_at - 1))

    factor_of = one(*pieces[0])
    for cut in pieces[1:]:
        factor_of = factor_of * one(*cut)
    return factor_of


def profile(number_of, total, reach, lean):
    weights = [(1 << 20) // math.isqrt(standing ** lean) + 1 for standing in range(2, number_of + 1)]
    surplus, given = total - reach - (number_of - 1), [1] * (number_of - 1)
    while surplus > 0:
        movable = [i for i in range(number_of - 1) if given[i] < reach]
        pool, left = sum([weights[i] for i in movable]), surplus
        for i in movable:
            extra = min(reach - given[i], max(1, left * weights[i] // pool), surplus)
            given[i] = given[i] + extra
            surplus = surplus - extra
    return np.array([reach] + given)


def ragged_sizes(key, number_of, total, bound, skew):
    if number_of == 2:
        one = jax.random.randint(key, (), max(1, total - bound), min(bound, total - 1) + 1)
        return jnp.stack([one, total - one])
    tallies = jnp.asarray(profile(number_of, total, bound, skew), jnp.int32)
    twos = (number_of - 1) // 2
    source_of, taker = tallies[1:1 + 2 * twos:2], tallies[2:2 + 2 * twos:2]
    margin = jnp.minimum(source_of - 1, bound - taker)
    shifted = jax.random.randint(jax.random.fold_in(key, 1), (twos,), 0, 1 << 20) % (margin + 1)
    tallies = tallies.at[1:1 + 2 * twos:2].set(source_of - shifted).at[2:2 + 2 * twos:2].set(taker + shifted)
    return tallies[jax.random.permutation(jax.random.fold_in(key, 2), number_of)]


def normal_values(rng, extent, spread, bound, split=(), kind=jnp.bfloat16):
    level = level_of(rng, extent, split, -0.22, 0.18) if split else 1.0
    result = jax.random.normal(rng, extent, jnp.float32) * spread * level
    return jnp.minimum(jnp.maximum(result, -bound), bound).astype(kind)


def setup_inputs(seed: int = 0) -> dict:
    seeds = jax.random.split(jax.random.key(seed), 14)
    inputs = normal_values(seeds[0], (TOKENS, D), 1.0, 6.0, ((0, 32),))
    segment_ids = jax.vmap(lambda own: jnp.searchsorted(jnp.cumsum(ragged_sizes(own, SEGS, TOK_DEV, SEQ_MOST, 2)), jnp.arange(TOK_DEV), side="right"))(jax.random.split(seeds[1], DEVICES)).reshape((DEVICES, TOK_DEV)).astype(jnp.int32)
    live_counts = draw_live_counts(jax.random.fold_in(seeds[13], 71), 0)
    cotangent = normal_values(seeds[3], (TOKENS, D), 1.0, 6.0, ((0, 32),))
    w_query = normal_values(seeds[4], (D, HEADS * HEAD), D ** -0.5, 0.25, ((0, 4),))
    w_key = normal_values(seeds[5], (D, KV_HEADS * HEAD), D ** -0.5, 0.25, ((0, 4),))
    w_value = normal_values(seeds[6], (D, KV_HEADS * HEAD), D ** -0.5, 0.25, ((0, 4),))
    w_out = normal_values(seeds[7], (HEADS * HEAD, D), (HEADS * HEAD // 8) ** -0.5, 0.75, ((1, 4),))
    w_gate = normal_values(seeds[8], (D, FF), D ** -0.5, 0.25, ((0, 4),))
    w_up = normal_values(seeds[9], (D, FF), D ** -0.5, 0.25, ((0, 4),))
    w_down = normal_values(seeds[10], (FF, D), FF ** -0.5, 0.15625, ((1, 4),))
    norm_attn = jnp.clip(1.0 + 0.1 * jax.random.normal(seeds[11], (D,), jnp.float32), 0.5, 1.5).astype(jnp.bfloat16)
    norm_ffn = jnp.clip(1.0 + 0.1 * jax.random.normal(seeds[12], (D,), jnp.float32), 0.5, 1.5).astype(jnp.bfloat16)
    return {"inputs": inputs, "segment_ids": segment_ids, "live_counts": live_counts, "cotangent": cotangent, "w_query": w_query, "w_key": w_key, "w_value": w_value, "w_out": w_out, "w_gate": w_gate, "w_up": w_up, "w_down": w_down, "norm_attn": norm_attn, "norm_ffn": norm_ffn}


norm_eps = 1e-05
rope_base = 100000.0
masked_value = -1e+30

def contract(pattern, left_op, right_op):
    return jnp.einsum(pattern, left_op.astype(jnp.float32), right_op.astype(jnp.float32))

def matmul(left_op, right_op):
    return jnp.dot(left_op, right_op, preferred_element_type=jnp.float32)

def rope_tables(segment_row):
    row_count = segment_row.shape[0]
    seg_first = jnp.searchsorted(segment_row, segment_row, side='left').astype(jnp.int32)
    offsets = (jnp.arange(row_count, dtype=jnp.int32) - seg_first).astype(jnp.float32)
    frequency = jnp.exp(jnp.arange(HEAD // 2, dtype=jnp.float32) * (-2.0 * math.log(rope_base) / HEAD))
    angles = offsets[:, None] * frequency[None, :]
    return (jnp.cos(angles)[:, None, :], jnp.sin(angles)[:, None, :])

def rotate(values, cosine, sine):
    half_size = values.shape[-1] // 2
    first_half = values[..., :half_size]
    second_half = values[..., half_size:]
    return jnp.concatenate([first_half * cosine - second_half * sine, second_half * cosine + first_half * sine], axis=-1)

def unrotate(values, cosine, sine):
    half_size = values.shape[-1] // 2
    first_half = values[..., :half_size]
    second_half = values[..., half_size:]
    return jnp.concatenate([first_half * cosine + second_half * sine, second_half * cosine - first_half * sine], axis=-1)

def norm_forward(values):
    inverse = lax.rsqrt(lax.optimization_barrier(jnp.mean(values * values, axis=-1, keepdims=True)) + norm_eps)
    return (values * inverse, inverse)

def norm_backward(grad_out, normed, gain, inverse):
    grad_normed = grad_out * gain
    grad_in = inverse * (grad_normed - normed * lax.optimization_barrier(jnp.mean(grad_normed * normed, axis=-1, keepdims=True)))
    return (grad_in, lax.optimization_barrier(jnp.sum(grad_out * normed, axis=0)))

def block_mask(segment_row, live_count, row_start, row_stop):
    position = jnp.arange(row_stop, dtype=jnp.int32)
    same_seq = segment_row[row_start:row_stop, None] == segment_row[None, :row_stop]
    causal = position[None, :] <= position[row_start:row_stop, None]
    key_ok = (position[None, :] < live_count) | (position[None, :] == position[row_start:row_stop, None])
    return same_seq & causal & key_ok

def attend(queries, keys_rot, values, segment_row, live_count):
    row_count = queries.shape[0]
    blk_size = min(512, row_count)
    score_scale = queries.shape[-1] ** (-0.5)
    out_blocks = []
    total_blocks = []
    for row_start in range(0, row_count, blk_size):
        row_stop = row_start + blk_size
        allowed = block_mask(segment_row, live_count, row_start, row_stop)
        head_outs = []
        head_totals = []
        for kv_group in range(keys_rot.shape[1]):
            scores = contract('qhd,kd->hqk', queries[row_start:row_stop, kv_group], keys_rot[:row_stop, kv_group]) * score_scale
            scores = jnp.where(allowed[None], scores, masked_value)
            row_max = lax.optimization_barrier(jnp.max(scores, axis=2, keepdims=True))
            log_total = row_max + jnp.log(lax.optimization_barrier(jnp.sum(jnp.exp(scores - row_max), axis=2, keepdims=True)))
            probs = jnp.exp(scores - log_total).astype(jnp.bfloat16)
            head_outs.append(contract('hqk,kd->qhd', probs, values[:row_stop, kv_group]).astype(jnp.bfloat16))
            head_totals.append(log_total[:, :, 0])
        out_blocks.append(jnp.stack(head_outs, axis=1))
        total_blocks.append(jnp.stack(head_totals, axis=0))
    return (jnp.concatenate(out_blocks, axis=0), jnp.concatenate(total_blocks, axis=2))

def attend_back(queries, keys_rot, values, segment_row, live_count, attn_out, log_totals, grad_attn):
    row_count = queries.shape[0]
    blk_size = min(512, row_count)
    score_scale = queries.shape[-1] ** (-0.5)
    deltas = lax.optimization_barrier(jnp.sum(grad_attn.astype(jnp.float32) * attn_out.astype(jnp.float32), axis=-1))
    grad_keys = jnp.zeros(keys_rot.shape, jnp.float32)
    grad_values = jnp.zeros(values.shape, jnp.float32)
    query_blocks = []
    for row_start in range(0, row_count, blk_size):
        row_stop = row_start + blk_size
        allowed = block_mask(segment_row, live_count, row_start, row_stop)
        head_grads = []
        for kv_group in range(keys_rot.shape[1]):
            query_blk = queries[row_start:row_stop, kv_group]
            grad_blk = grad_attn[row_start:row_stop, kv_group]
            scores = contract('qhd,kd->hqk', query_blk, keys_rot[:row_stop, kv_group]) * score_scale
            scores = jnp.where(allowed[None], scores, masked_value)
            probs = jnp.exp(scores - log_totals[kv_group][:, row_start:row_stop, None])
            probs_bf = probs.astype(jnp.bfloat16)
            grad_probs = contract('qhd,kd->hqk', grad_blk, values[:row_stop, kv_group])
            delta_blk = jnp.transpose(deltas[row_start:row_stop, kv_group])
            grad_scores = (probs * (grad_probs - delta_blk[:, :, None]) * score_scale).astype(jnp.bfloat16)
            head_grads.append(contract('hqk,kd->qhd', grad_scores, keys_rot[:row_stop, kv_group]))
            grad_keys = grad_keys.at[:row_stop, kv_group].add(contract('hqk,qhd->kd', grad_scores, query_blk))
            grad_values = grad_values.at[:row_stop, kv_group].add(contract('hqk,qhd->kd', probs_bf, grad_blk))
        query_blocks.append(jnp.stack(head_grads, axis=1))
    return (jnp.concatenate(query_blocks, axis=0), grad_keys, grad_values)

def layer_forward(inputs, segment_row, live_count, weights):
    w_query, w_key, w_value, w_out, w_gate, w_up, w_down, norm_attn, norm_ffn = weights
    row_count = inputs.shape[0]
    group_size = HEADS // KV_HEADS
    live_rows = jnp.arange(row_count, dtype=jnp.int32) < live_count
    input_f = inputs.astype(jnp.float32)
    normed_one, inverse_one = norm_forward(input_f)
    hidden_one = (normed_one * norm_attn.astype(jnp.float32)).astype(jnp.bfloat16)
    cosine, sine = rope_tables(segment_row)
    query_raw = matmul(hidden_one, w_query).reshape(row_count, HEADS, HEAD)
    key_raw = matmul(hidden_one, w_key).reshape(row_count, KV_HEADS, HEAD)
    value_bf = matmul(hidden_one, w_value).astype(jnp.bfloat16).reshape(row_count, KV_HEADS, HEAD)
    query_rot = rotate(query_raw, cosine, sine).astype(jnp.bfloat16).reshape(row_count, KV_HEADS, group_size, HEAD)
    key_rot = rotate(key_raw, cosine, sine).astype(jnp.bfloat16)
    attn_out, log_totals = attend(query_rot, key_rot, value_bf, segment_row, live_count)
    attn_flat = attn_out.reshape(row_count, HEADS * HEAD)
    mid_f = input_f + matmul(attn_flat, w_out)
    normed_two, inverse_two = norm_forward(mid_f)
    hidden_two = (normed_two * norm_ffn.astype(jnp.float32)).astype(jnp.bfloat16)
    gate_pre = matmul(hidden_two, w_gate)
    up_pre = matmul(hidden_two, w_up)
    sigmoid_gate = jax.nn.sigmoid(gate_pre)
    silu_gate = gate_pre * sigmoid_gate
    mixed = (silu_gate * up_pre).astype(jnp.bfloat16)
    output = jnp.where(live_rows[:, None], mid_f + matmul(mixed, w_down), 0.0).astype(jnp.bfloat16)
    saved = (segment_row, live_count, live_rows, normed_one, inverse_one, hidden_one, cosine, sine, query_rot, key_rot, value_bf, attn_out, log_totals, attn_flat, normed_two, inverse_two, hidden_two, gate_pre, up_pre, sigmoid_gate, silu_gate, mixed)
    return (output, saved)

def layer_backward(saved, cotangent, weights, grad_scale):
    w_query, w_key, w_value, w_out, w_gate, w_up, w_down, norm_attn, norm_ffn = weights
    segment_row, live_count, live_rows, normed_one, inverse_one, hidden_one, cosine, sine, query_rot, key_rot, value_bf, attn_out, log_totals, attn_flat, normed_two, inverse_two, hidden_two, gate_pre, up_pre, sigmoid_gate, silu_gate, mixed = saved
    row_count = cotangent.shape[0]
    group_size = HEADS // KV_HEADS
    cot = jnp.where(live_rows[:, None], cotangent, jnp.zeros_like(cotangent))
    grad_down = matmul(mixed.T, cot) * grad_scale
    grad_mixed = matmul(cot, w_down.T)
    grad_gate_pre = (grad_mixed * up_pre * (sigmoid_gate * (1.0 + gate_pre * (1.0 - sigmoid_gate)))).astype(jnp.bfloat16)
    grad_up_pre = (grad_mixed * silu_gate).astype(jnp.bfloat16)
    grad_gate = matmul(hidden_two.T, grad_gate_pre) * grad_scale
    grad_up = matmul(hidden_two.T, grad_up_pre) * grad_scale
    grad_hidden_two = matmul(grad_gate_pre, w_gate.T) + matmul(grad_up_pre, w_up.T)
    grad_mid_norm, grad_norm_ffn = norm_backward(grad_hidden_two, normed_two, norm_ffn.astype(jnp.float32), inverse_two)
    grad_mid = cot.astype(jnp.float32) + grad_mid_norm
    grad_mid_bf = grad_mid.astype(jnp.bfloat16)
    grad_out_w = matmul(attn_flat.T, grad_mid_bf) * grad_scale
    grad_attn = matmul(grad_mid_bf, w_out.T).astype(jnp.bfloat16).reshape(row_count, KV_HEADS, group_size, HEAD)
    grad_query_rot, grad_key_rot, grad_value_f = attend_back(query_rot, key_rot, value_bf, segment_row, live_count, attn_out, log_totals, grad_attn)
    grad_query_raw = unrotate(grad_query_rot.reshape(row_count, HEADS, HEAD), cosine, sine).astype(jnp.bfloat16).reshape(row_count, HEADS * HEAD)
    grad_key_raw = unrotate(grad_key_rot, cosine, sine).astype(jnp.bfloat16).reshape(row_count, KV_HEADS * HEAD)
    grad_value_bf = grad_value_f.astype(jnp.bfloat16).reshape(row_count, KV_HEADS * HEAD)
    grad_query_w = matmul(hidden_one.T, grad_query_raw) * grad_scale
    grad_key_w = matmul(hidden_one.T, grad_key_raw) * grad_scale
    grad_value_w = matmul(hidden_one.T, grad_value_bf) * grad_scale
    grad_hidden_one = matmul(grad_query_raw, w_query.T) + matmul(grad_key_raw, w_key.T) + matmul(grad_value_bf, w_value.T)
    grad_in_norm, grad_norm_attn = norm_backward(grad_hidden_one, normed_one, norm_attn.astype(jnp.float32), inverse_one)
    grad_input = grad_mid + grad_in_norm
    return (grad_input, (grad_query_w, grad_key_w, grad_value_w, grad_out_w, grad_gate, grad_up, grad_down, grad_norm_attn * grad_scale, grad_norm_ffn * grad_scale))

def reference(inputs, segment_ids, live_counts, cotangent, w_query, w_key, w_value, w_out, w_gate, w_up, w_down, norm_attn, norm_ffn):
    weights = (w_query, w_key, w_value, w_out, w_gate, w_up, w_down, norm_attn, norm_ffn)
    grad_scale = float(TOKENS) ** (-0.5)

    def scan_step(running, block_data):
        input_blk, segment_row, live_count, cot_blk = block_data
        output_blk, saved = layer_forward(input_blk, segment_row, live_count, weights)
        grad_blk, block_grads = layer_backward(saved, cot_blk, weights, grad_scale)
        summed = tuple((total_now + term_now for total_now, term_now in zip(running, block_grads)))
        return (summed, (output_blk, grad_blk))
    zero_grads = tuple((jnp.zeros(weight_now.shape, jnp.float32) for weight_now in weights))
    totals, (outputs, grad_inputs) = lax.scan(scan_step, zero_grads, (inputs.reshape(DEVICES, TOK_DEV, D), segment_ids, live_counts.astype(jnp.int32), cotangent.reshape(DEVICES, TOK_DEV, D)))
    return (outputs.reshape(TOKENS, D), grad_inputs.reshape(TOKENS, D), totals[0], totals[1], totals[2], totals[3], totals[4], totals[5], totals[6], totals[7], totals[8])
```

```python
import math

import jax
import jax.numpy as jnp
from jax import lax
from jax.experimental import pallas as pl
from jax.experimental.pallas import tpu as pltpu
from jax.sharding import PartitionSpec as P

HEADS = 9
KV_HEADS = 3
HEAD = 64
WIDTH = 576
FF = 1536
QKV = 960
CH = 256
NCH = 25
FF_CH = 6
G_OUT = 18
G_QKV = 20
G_TAIL = 24
W_TAIL = 0
W_QKV = 1
W_OUT = 5
W_FF = 7
LAG = 2

norm_eps = 1e-05
rope_base = 100000.0
masked_value = -1e30
MESH = pl.DeviceIdType.MESH
f32 = jnp.float32
bf16 = jnp.bfloat16


def nn(a, b):
    return lax.dot_general(a, b, (((1,), (0,)), ((), ())), preferred_element_type=f32)


def nt(a, b):
    return lax.dot_general(a, b, (((1,), (1,)), ((), ())), preferred_element_type=f32)


def tn(a, b):
    return lax.dot_general(a, b, (((0,), (0,)), ((), ())), preferred_element_type=f32)


class Where:
    def __init__(self, shard, chain):
        self.rep = lax.axis_index("replica")
        self.grp = lax.axis_index("group")
        self.core = lax.rem(self.grp, 2)
        self.y = lax.div(self.grp, 2)
        self.xp = lax.rem(self.rep, 2)
        self.q = lax.div(self.rep, 2)
        self.core_peer = (self.rep, self.y * 2 + 1 - self.core)
        self.y_peer = (self.rep, (1 - self.y) * 2 + self.core)
        self.x_peer = (self.rep + 1 - 2 * self.xp, self.grp)
        self.left = (self.rep - 2, self.grp)
        self.right = (self.rep + 2, self.grp)
        self.shard = shard
        self.chain = chain

    def rows(self, y, core):
        return pl.ds(pl.multiple_of((y * 2 + core) * self.shard, 16), self.shard)


def enter(w, use_chain):
    barrier = pltpu.get_barrier_semaphore()
    for peer in (w.core_peer, w.y_peer, w.x_peer):
        pl.semaphore_signal(barrier, inc=1, device_id=peer, device_id_type=MESH)
    if use_chain:
        for step in (1, w.chain - 1):
            peer = (lax.rem(w.q + step, w.chain) * 2 + w.xp, w.grp)
            pl.semaphore_signal(barrier, inc=1, device_id=peer, device_id_type=MESH)
    pl.semaphore_wait(barrier, 5 if use_chain else 3)


def remote(src, dst, send, recv, peer):
    return pltpu.make_async_remote_copy(
        src_ref=src, dst_ref=dst, send_sem=send, recv_sem=recv, device_id=peer, device_id_type=MESH
    )


class Gather:
    def __init__(self, w, own, full, sems):
        self.w, self.own, self.full = w, own, full
        self.s1, self.r1, self.s2, self.r2, self.sy, self.sx, self.ryx = sems
        self.mine = w.grp
        self.other = (1 - w.y) * 2 + w.core

    def core_own(self, k):
        return remote(
            self.own.at[k],
            self.full.at[self.mine, k],
            self.s1.at[k],
            self.r1.at[k],
            self.w.core_peer,
        )

    def y_own(self, k):
        return remote(
            self.own.at[k],
            self.full.at[self.mine, k],
            self.sy.at[k],
            self.ryx.at[k],
            self.w.y_peer,
        )

    def x_fwd(self, k):
        block = self.full.at[self.other, k]
        return remote(block, block, self.sx.at[k], self.ryx.at[k], self.w.x_peer)

    def core_fwd(self, k):
        block = self.full.at[self.other, k]
        return remote(block, block, self.s2.at[k], self.r2.at[k], self.w.core_peer)

    def start(self):
        @pl.loop(0, NCH)
        def _(k):
            @pl.when(lax.rem(k, 2) == self.w.xp)
            def _():
                self.y_own(k).start()

            self.core_own(k).start()
            self.full[self.mine, k] = self.own[k]

    def relay(self, j):
        near = 2 * j + self.w.xp
        far = 2 * (j - LAG) + 1 - self.w.xp

        @pl.when(near < NCH)
        def _():
            self.y_own(near).wait_recv()
            self.x_fwd(near).start()
            self.core_fwd(near).start()

        @pl.when((far >= 0) & (far < NCH))
        def _():
            self.x_fwd(far).wait_recv()
            self.core_fwd(far).start()

    def ready(self, k):
        self.core_own(k).wait_recv()
        self.core_fwd(k).wait_recv()

    def drain(self):
        @pl.loop(0, NCH)
        def _(k):
            self.core_own(k).wait_send()
            self.core_fwd(k).wait_send()

            @pl.when(lax.rem(k, 2) == self.w.xp)
            def _():
                self.y_own(k).wait_send()
                self.x_fwd(k).wait_send()


class Reduce:
    def __init__(self, w, grads, total, bufs, sems, scale):
        self.w, self.g, self.o, self.scale = w, grads, total, scale
        self.ra, self.sb, self.rb, self.tc, self.rc, self.pr, self.rl, self.pq, self.rr = bufs
        (
            self.sa,
            self.rsa,
            self.ssb,
            self.rsb,
            self.ssc,
            self.rsc,
            self.ssr,
            self.rsr,
            self.ssl,
            self.rsl,
        ) = sems

    def core_send(self, side, k):
        return remote(
            self.g.at[k, self.w.rows(side, 1 - self.w.core), :],
            self.ra.at[side, k],
            self.sa.at[side, k],
            self.rsa.at[side, k],
            self.w.core_peer,
        )

    def y_send(self, k):
        return remote(
            self.sb.at[k], self.rb.at[k], self.ssb.at[k], self.rsb.at[k], self.w.y_peer
        )

    def x_send(self, k):
        return remote(
            self.tc.at[k], self.rc.at[k], self.ssc.at[k], self.rsc.at[k], self.w.x_peer
        )

    def right_send(self, k):
        return remote(
            self.pr.at[k], self.rl.at[k], self.ssr.at[k], self.rsr.at[k], self.w.right
        )

    def left_send(self, k):
        return remote(self.pq.at[k], self.rr.at[k], self.ssl.at[k], self.rsl.at[k], self.w.left)

    def first(self, k):
        self.core_send(0, k).start()
        self.core_send(1, k).start()

    def steps(self):
        return NCH + LAG * 2 + LAG * (self.w.chain - 1)

    def step(self, t):
        w = self.w

        def at(k, body):
            pl.when((k >= 0) & (k < NCH))(lambda: body(k))

        def stage_y(k):
            self.core_send(0, k).wait_recv()
            self.core_send(1, k).wait_recv()
            away = self.g[k, w.rows(1 - w.y, w.core), :].astype(f32) + self.ra[1 - w.y, k].astype(
                f32
            )
            self.sb[k] = away.astype(bf16)
            self.y_send(k).start()
            self.o[k] = self.g[k, w.rows(w.y, w.core), :].astype(f32) + self.ra[w.y, k].astype(f32)

        def stage_x(k):
            self.y_send(k).wait_recv()
            total = self.o[k] + self.rb[k].astype(f32)
            self.tc[k] = total.astype(bf16)
            self.x_send(k).start()

        def stage_pair(k):
            self.x_send(k).wait_recv()
            self.o[k] = self.tc[k].astype(f32) + self.rc[k].astype(f32)

        def stage_right(k):
            @pl.when(w.q > 0)
            def _():
                self.right_send(k).wait_recv()

            @pl.when((w.q > 0) & (w.q < w.chain - 1))
            def _():
                self.pr[k] = (self.o[k] + self.rl[k].astype(f32)).astype(bf16)

            @pl.when(w.q == 0)
            def _():
                self.pr[k] = self.o[k].astype(bf16)

            @pl.when(w.q < w.chain - 1)
            def _():
                self.right_send(k).start()

        def stage_left(k):
            @pl.when(w.q < w.chain - 1)
            def _():
                self.left_send(k).wait_recv()

            @pl.when((w.q > 0) & (w.q < w.chain - 1))
            def _():
                self.pq[k] = (self.o[k] + self.rr[k].astype(f32)).astype(bf16)

            @pl.when(w.q == w.chain - 1)
            def _():
                self.pq[k] = self.o[k].astype(bf16)

            @pl.when(w.q > 0)
            def _():
                self.left_send(k).start()

        def stage_last(k):
            @pl.when(w.q > 0)
            def _():
                self.o[k] = self.o[k] + self.rl[k].astype(f32)

            @pl.when(w.q < w.chain - 1)
            def _():
                self.o[k] = self.o[k] + self.rr[k].astype(f32)

            self.o[k] = self.o[k] * self.scale

        at(t, stage_y)
        at(t - LAG, stage_x)
        at(t - 2 * LAG, stage_pair)
        at(t - 2 * LAG - LAG * w.q, stage_right)
        at(t - 2 * LAG - LAG * (w.chain - 1 - w.q), stage_left)
        at(t - 2 * LAG - LAG * (w.chain - 1), stage_last)

    def drain(self):
        w = self.w

        @pl.loop(0, NCH)
        def _(k):
            self.core_send(0, k).wait_send()
            self.core_send(1, k).wait_send()
            self.y_send(k).wait_send()
            self.x_send(k).wait_send()

            @pl.when(w.q < w.chain - 1)
            def _():
                self.right_send(k).wait_send()

            @pl.when(w.q > 0)
            def _():
                self.left_send(k).wait_send()


def rope(values, cosine, sine, sign):
    lane = lax.broadcasted_iota(jnp.int32, values.shape, 1)
    low = lax.rem(lane, HEAD) < HEAD // 2
    swapped = jnp.where(
        low, pltpu.roll(values, 128 - HEAD // 2, 1), pltpu.roll(values, HEAD // 2, 1)
    )
    return values * cosine + swapped * jnp.where(low, -sign * sine, sign * sine)


def compute(
    wait_w,
    give_g,
    x_ref,
    cot_ref,
    seg_row,
    seg_col,
    live_ref,
    w_ref,
    out_ref,
    gin_ref,
    g_ref,
    raw,
    qkv,
    attn,
    gattn,
    probs,
    gqkv,
    mids,
    mixes,
):
    rows = x_ref.shape[0]

    def wt(k):
        return w_ref[:, k].reshape(WIDTH, CH)

    live = live_ref[0, 0]
    pos_row = lax.broadcasted_iota(jnp.int32, (rows, rows), 1)
    pos_col = lax.broadcasted_iota(jnp.int32, (rows, rows), 0)
    keys, queries = seg_row[...], seg_col[...]
    allowed = (
        (keys == queries)
        & (pos_row <= pos_col)
        & ((pos_row < live) | (pos_row == pos_col))
    )
    first = jnp.sum(jnp.where(keys < queries, 1.0, 0.0).astype(f32), axis=1, keepdims=True)
    lane = lax.broadcasted_iota(jnp.int32, (rows, 128), 1)
    index = lax.broadcasted_iota(jnp.int32, (rows, 128), 0).astype(f32)
    freq = jnp.exp(
        lax.rem(lane, HEAD // 2).astype(f32) * (-2.0 * math.log(rope_base) / HEAD)
    )
    angle = (index - first) * freq
    cosine, sine = jnp.cos(angle), jnp.sin(angle)

    xf = x_ref[...].astype(f32)
    r1 = lax.rsqrt(jnp.mean(xf * xf, axis=-1, keepdims=True) + norm_eps)
    n1 = xf * r1
    wait_w(W_TAIL)
    gains = wt(W_TAIL)[:, 128:256].astype(f32).T
    gain1, gain2 = gains[0:1, :], gains[64:65, :]
    h1 = (n1 * gain1).astype(bf16)
    for j in range(4):
        wait_w(W_QKV + j)
        raw[:, j * CH : (j + 1) * CH] = nn(h1, wt(W_QKV + j))
    for j in range(6):
        qkv[:, j * 128 : (j + 1) * 128] = rope(
            raw[:, j * 128 : (j + 1) * 128], cosine, sine, 1.0
        ).astype(bf16)
    qkv[:, 768:1024] = raw[:, 768:1024].astype(bf16)

    score_scale = HEAD ** (-0.5)

    def head(ref, at):
        return ref[:, at * HEAD : (at + 1) * HEAD]

    for h in range(HEADS):
        kv = h // 3
        s = nt(head(qkv, h), head(qkv, HEADS + kv)) * score_scale
        s = jnp.where(allowed, s, masked_value)
        e = jnp.exp(s - jnp.max(s, axis=1, keepdims=True))
        p = e * (1.0 / jnp.sum(e, axis=1, keepdims=True))
        probs[h] = p
        attn[:, h * HEAD : (h + 1) * HEAD] = nn(
            p.astype(bf16), head(qkv, HEADS + KV_HEADS + kv)
        ).astype(bf16)

    wait_w(W_OUT)
    wait_w(W_OUT + 1)
    mid = (
        xf
        + nt(attn[:, 0:256], wt(W_OUT))
        + nt(attn[:, 256:512], wt(W_OUT + 1))
        + nt(attn[:, 512:576], wt(W_TAIL)[:, 0:64])
    )
    r2 = lax.rsqrt(jnp.mean(mid * mid, axis=-1, keepdims=True) + norm_eps)
    n2 = mid * r2
    h2 = (n2 * gain2).astype(bf16)
    h2t = h2.T
    live_rows = lax.broadcasted_iota(jnp.int32, (rows, 1), 0) < live
    cot_f = jnp.where(live_rows, cot_ref[...].astype(f32), 0.0)
    cot = cot_f.astype(bf16)
    cott = cot.T

    mids[...] = mid
    gh2 = jnp.zeros((rows, WIDTH), f32)
    for j in range(FF_CH):
        kd, kg, ku = W_FF + 3 * j, W_FF + 3 * j + 1, W_FF + 3 * j + 2
        wait_w(kd)
        wait_w(kg)
        wait_w(ku)
        gate = nn(h2, wt(kg))
        up = nn(h2, wt(ku))
        gm = nn(cot, wt(kd))
        sig = 1.0 / (1.0 + jnp.exp(-gate))
        silu = gate * sig
        mixed = (silu * up).astype(bf16)
        mixes[:, j * CH : (j + 1) * CH] = mixed
        g_ref[3 * j] = nn(cott, mixed).astype(bf16)
        give_g(3 * j)
        ggate = (gm * up * (sig * (1.0 + gate * (1.0 - sig)))).astype(bf16)
        gup = (gm * silu).astype(bf16)
        g_ref[3 * j + 1] = nn(h2t, ggate).astype(bf16)
        give_g(3 * j + 1)
        g_ref[3 * j + 2] = nn(h2t, gup).astype(bf16)
        give_g(3 * j + 2)
        gh2 = gh2 + nt(ggate, wt(kg)) + nt(gup, wt(ku))

    gn = gh2 * gain2
    gmid = cot_f + r2 * (gn - n2 * jnp.mean(gn * n2, axis=-1, keepdims=True))
    ggain2 = jnp.sum(gh2 * n2, axis=0, keepdims=True)
    gmid_bf = gmid.astype(bf16)
    gmidt = gmid_bf.T
    for j in range(2):
        g_ref[G_OUT + j] = nn(gmidt, attn[:, j * CH : (j + 1) * CH]).astype(bf16)
        give_g(G_OUT + j)
        gattn[:, j * CH : (j + 1) * CH] = nn(gmid_bf, wt(W_OUT + j)).astype(bf16)
    gattn[:, 512:576] = nn(gmid_bf, wt(W_TAIL)[:, 0:64]).astype(bf16)
    tail_grad = nn(gmidt, attn[:, 512:640]).astype(bf16)

    for kv in range(KV_HEADS):
        gk = jnp.zeros((rows, HEAD), f32)
        gv = jnp.zeros((rows, HEAD), f32)
        for h in range(3 * kv, 3 * kv + 3):
            ga = head(gattn, h)
            p = probs[h]
            delta = jnp.sum(
                ga.astype(f32) * head(attn, h).astype(f32), axis=1, keepdims=True
            )
            gp = nt(ga, head(qkv, HEADS + KV_HEADS + kv))
            gs = (p * (gp - delta) * score_scale).astype(bf16)
            raw[:, h * HEAD : (h + 1) * HEAD] = nn(gs, head(qkv, HEADS + kv))
            gk = gk + tn(gs, head(qkv, h))
            gv = gv + tn(p.astype(bf16), ga)
        raw[:, (HEADS + kv) * HEAD : (HEADS + kv + 1) * HEAD] = gk
        at = HEADS + KV_HEADS + kv
        raw[:, at * HEAD : (at + 1) * HEAD] = gv
    raw[:, QKV:1024] = jnp.zeros((rows, 1024 - QKV), f32)
    for j in range(6):
        gqkv[:, j * 128 : (j + 1) * 128] = rope(
            raw[:, j * 128 : (j + 1) * 128], cosine, sine, -1.0
        ).astype(bf16)
    gqkv[:, 768:1024] = raw[:, 768:1024].astype(bf16)
    h1t = h1.T
    gh1 = jnp.zeros((rows, WIDTH), f32)
    for j in range(4):
        block = gqkv[:, j * CH : (j + 1) * CH]
        g_ref[G_QKV + j] = nn(h1t, block).astype(bf16)
        give_g(G_QKV + j)
        gh1 = gh1 + nt(block, wt(W_QKV + j))
    gm1 = gh1 * gain1
    gin_ref[...] = gmid + r1 * (gm1 - n1 * jnp.mean(gm1 * n1, axis=-1, keepdims=True))
    ggain1 = jnp.sum(gh1 * n1, axis=0, keepdims=True)
    which = lax.broadcasted_iota(jnp.int32, (128, WIDTH), 0) < 64
    gain_grads = jnp.where(which, ggain1, ggain2).T
    g_ref[G_TAIL, :, 0:128] = tail_grad
    g_ref[G_TAIL, :, 128:256] = gain_grads.astype(bf16)
    give_g(G_TAIL)
    for j in range(FF_CH):
        mids[...] += nt(mixes[:, j * CH : (j + 1) * CH], wt(W_FF + 3 * j))
    out_ref[...] = jnp.where(live_rows, mids[...], 0.0).astype(bf16)


def compute_scratch(rows):
    return [
        pltpu.VMEM((rows, 1024), f32),
        pltpu.VMEM((rows, 1024), bf16),
        pltpu.VMEM((rows, 640), bf16),
        pltpu.VMEM((rows, 640), bf16),
        pltpu.VMEM((HEADS, rows, rows), f32),
        pltpu.VMEM((rows, 1024), bf16),
        pltpu.VMEM((rows, WIDTH), f32),
        pltpu.VMEM((rows, FF), bf16),
    ]


def dma(*shape):
    return pltpu.SemaphoreType.DMA(shape)


def gather_kernel(chain, own, full, *sems):
    w = Where(own.shape[1], chain)
    enter(w, False)
    gather = Gather(w, own, full, sems)
    gather.start()

    @pl.loop(0, (NCH + 1) // 2 + LAG)
    def _(j):
        gather.relay(j)

    @pl.loop(0, NCH)
    def _(k):
        gather.ready(k)

    gather.drain()


def reduce_kernel(chain, scale, grads, total, *rest):
    w = Where(total.shape[1], chain)
    enter(w, True)
    red = Reduce(w, grads, total, rest[:9], rest[9:], scale)

    @pl.loop(0, NCH)
    def _(k):
        red.first(k)

    @pl.loop(0, red.steps())
    def _(t):
        red.step(t)

    red.drain()


def compute_kernel(x, cot, srow, scol, live, w, out, gin, g, *scratch):
    scratch[2][:, 512:640] = jnp.zeros((x.shape[0], 128), bf16)
    compute(
        lambda k: None, lambda k: None, x, cot, srow, scol, live, w, out, gin, g, *scratch
    )


def pack(w_query, w_key, w_value, w_out, w_gate, w_up, w_down, norm_attn, norm_ffn):
    shard = w_query.shape[0]

    def split(matrix):
        return jnp.transpose(matrix.reshape(shard, -1, CH), (1, 0, 2))

    out_t = w_out.T
    wide = jnp.concatenate(
        [w_query, w_key, w_value, jnp.zeros((shard, 1024 - QKV), bf16)], axis=1
    )
    tail = jnp.concatenate(
        [
            out_t[:, 512:576],
            jnp.zeros((shard, 64), bf16),
            jnp.broadcast_to(norm_attn[:, None], (shard, 64)),
            jnp.broadcast_to(norm_ffn[:, None], (shard, 64)),
        ],
        axis=1,
    )
    ff = jnp.stack([split(w_down.T), split(w_gate), split(w_up)], axis=1)
    return jnp.concatenate(
        [tail[None], split(wide), split(out_t[:, :512]), ff.reshape(3 * FF_CH, shard, CH)],
        axis=0,
    )


def unpack(total):
    shard = total.shape[1]

    def join(chunks):
        return jnp.transpose(chunks, (1, 0, 2)).reshape(shard, -1)

    ff = total[: 3 * FF_CH].reshape(FF_CH, 3, shard, CH)
    qkv = join(total[G_QKV : G_QKV + 4])
    tail = total[G_TAIL]
    out_t = jnp.concatenate([join(total[G_OUT : G_OUT + 2]), tail[:, :64]], axis=1)
    return (
        qkv[:, :576],
        qkv[:, 576:768],
        qkv[:, 768:960],
        out_t.T,
        join(ff[:, 1]),
        join(ff[:, 2]),
        join(ff[:, 0]).T,
        tail[:, 128],
        tail[:, 192],
    )


def local(inputs, segment_ids, live_counts, cotangent, *weights):
    rows = inputs.shape[0]
    chain = lax.axis_size("replica") // 2
    token_total = rows * lax.axis_size("replica") * lax.axis_size("group")
    scale = float(token_total) ** (-0.5)
    own = pack(*weights)
    shard = own.shape[1]
    vmem = pl.BlockSpec(memory_space=pltpu.VMEM)

    full = pl.pallas_call(
        lambda *refs: gather_kernel(chain, *refs),
        out_shape=jax.ShapeDtypeStruct((4, NCH, shard, CH), bf16),
        in_specs=[vmem],
        out_specs=vmem,
        scratch_shapes=[dma(NCH)] * 7,
        compiler_params=pltpu.CompilerParams(
            collective_id=0, has_side_effects=True, vmem_limit_bytes=60 << 20
        ),
        name="gather",
    )(own)
    output, grad_input, grads = pl.pallas_call(
        compute_kernel,
        out_shape=(
            jax.ShapeDtypeStruct((rows, WIDTH), bf16),
            jax.ShapeDtypeStruct((rows, WIDTH), f32),
            jax.ShapeDtypeStruct((NCH, WIDTH, CH), bf16),
        ),
        in_specs=[vmem] * 4 + [pl.BlockSpec(memory_space=pltpu.SMEM), vmem],
        out_specs=(
            pl.BlockSpec((rows, WIDTH), lambda: (0, 0)),
            pl.BlockSpec((rows, WIDTH), lambda: (0, 0)),
            vmem,
        ),
        scratch_shapes=compute_scratch(rows),
        compiler_params=pltpu.CompilerParams(vmem_limit_bytes=60 << 20),
        name="layer",
    )(
        inputs,
        cotangent,
        segment_ids,
        segment_ids.reshape(rows, 1),
        live_counts.reshape(1, 1),
        full,
    )
    buf = pltpu.VMEM((NCH, shard, CH), bf16)
    total = pl.pallas_call(
        lambda *refs: reduce_kernel(chain, scale, *refs),
        out_shape=jax.ShapeDtypeStruct((NCH, shard, CH), f32),
        in_specs=[vmem],
        out_specs=vmem,
        scratch_shapes=[pltpu.VMEM((2, NCH, shard, CH), bf16)]
        + [buf] * 8
        + [dma(2, NCH)] * 2
        + [dma(NCH)] * 8,
        compiler_params=pltpu.CompilerParams(
            collective_id=1, has_side_effects=True, vmem_limit_bytes=60 << 20
        ),
        name="reduce",
    )(grads)
    return (output, grad_input) + unpack(total)


def solution(mesh):
    rows = P(("replica", "group"), None)
    weight = [P("group", None)] * 3 + [P(None, "group")] + [P("group", None)] * 2
    weight = weight + [P(None, "group"), P("group"), P("group")]
    return jax.shard_map(
        local,
        mesh=mesh,
        in_specs=(rows, rows, P(("replica", "group")), rows, *weight),
        out_specs=(rows, rows, *weight),
        check_vma=False,
    )
```
